512 devices in a mesh: span: 16 (over z, core), stream: 32 (over x, y).
Axes of the slice: x: 4, y: 8, z: 8, core: 2. Of those that a mesh axis runs over, the one named last changes fastest.
Arguments:
- right_side: float32 [64, 1048576], P(None, ('span', 'stream')), may hold values from -6 to 6
- start_guess: float32 [64, 1048576], P(None, ('span', 'stream')), may hold values from -6 to 6
- fine_matrix: bfloat16 [8192, 5, 128, 128], P(('span', 'stream'))
- fine_columns: int32 [8192, 5], P(('span', 'stream')), may hold values from 0 to 31, as said below
- send_lists: int32 [512, 16], P(('span', 'stream')), may hold values from 0 to 15
- aggregates: int32 [1048576], P(('span', 'stream')), may hold values from 0 to 127
- coarse_matrix: float32 [512, 5, 128, 128], P(('span', 'stream'))
Outputs:
- solution: float32 [64, 1048576], P(None, ('span', 'stream'))
- coarse_correction: float32 [64, 65536], P(None, ('span', 'stream'))
The draws below stay inside these ranges and needn't reach their ends.
Inputs may be any that keep to these rules, and one draw needn't show every extreme that they name: `fine_columns`: entry 0 of each block row is the row block itself (its local index); the entries of one block row are distinct; entries below 16 name local blocks, entry 16 + d * 4 + h names received slot h from neighbour d; on every device every received slot is named by some block row.
All inputs are finite; a program needn't handle non-finite values.
Results may differ from the reference program's by a relative error of at most 0.0003.
Values sent between devices are 32-bit elements; how exact they have to be, the bound alone decides.
A program may use at most 64 MiB of HBM per device.

```python
import jax
import jax.numpy as jnp
from jax import lax

BS = 128
RB = 16
NNZB = 5
HB = 4
NV = 64
ROWBLOCKS = 8192
ROWS = 1048576
CROWS = 65536
N_SPAN = 16
N_STREAM = 32
DEVICES = 512


def matrix_draw(key, shape, spread):
    key_noise, key_diag = jax.random.split(key, 2)
    noise = jnp.clip(jax.random.normal(key_noise, shape, jnp.float32), -4.0, 4.0)
    size_one = shape[2]
    inner = shape[1]
    same = jnp.arange(size_one)[:, None] == jnp.arange(size_one)[None, :]
    first = (jnp.arange(inner) == 0)[:, None, None]
    identity = jnp.logical_and(same[None, :, :], first).astype(jnp.float32)
    diag_values = 1.5 + 2.5 * jax.random.uniform(key_diag, (shape[0], 1, size_one, 1), jnp.float32)
    result = noise * spread + identity[None] * diag_values
    return result.astype(jnp.float32)


def draw_fine_matrix(key, part):
    return matrix_draw(key, (ROWBLOCKS, NNZB, BS, BS), 0.8 / (NNZB * BS) ** 0.5).astype(jnp.bfloat16)


def draw_coarse_matrix(key, part):
    return matrix_draw(key, (DEVICES, 5, BS, BS), 0.8 / (5 * BS) ** 0.5)


def device_columns(key):
    key_rows, key_rest = jax.random.split(key)
    row_order = jax.random.permutation(key_rows, RB).astype(jnp.int32)
    slot_of_row = jnp.full((RB,), -1, jnp.int32).at[row_order[:4 * HB]].set(jnp.arange(4 * HB, dtype=jnp.int32))
    row_keys = jax.random.split(key_rest, RB)
    perms = jax.vmap(lambda one: jax.random.permutation(one, RB - 1))(row_keys).astype(jnp.int32)
    rows = jnp.arange(RB, dtype=jnp.int32)
    others = (rows[:, None] + 1 + perms) % RB
    has_slot = slot_of_row >= 0
    leading = jnp.where(has_slot, RB + slot_of_row, others[:, 0])
    if NNZB > 2:
        trailing = jnp.where(has_slot[:, None], others[:, :NNZB - 2], others[:, 1:NNZB - 1])
        return jnp.concatenate([rows[:, None], leading[:, None], trailing], 1).astype(jnp.int32)
    return jnp.concatenate([rows[:, None], leading[:, None]], 1).astype(jnp.int32)


def draw_fine_columns(key, part):
    keys = jax.random.split(key, DEVICES)
    return jax.vmap(device_columns)(keys).reshape(ROWBLOCKS, NNZB).astype(jnp.int32)


def touch_ends(drawn, rng, least, largest):
    index_at = [jax.random.randint(jax.random.fold_in(rng, axis), (), 0, length) for axis, length in enumerate(drawn.shape)]
    longest = drawn.shape.index(max(drawn.shape))
    neighbour = index_at[:longest] + [(index_at[longest] + 1) % drawn.shape[longest]] + index_at[longest + 1:]
    return drawn.at[tuple(index_at)].set(least).at[tuple(neighbour)].set(largest)


def steps_of(key, extent, cuts, low, largest):
    level, own = 1.0, jax.random.fold_in(key, 6)
    for axis_at, blocks in cuts:
        draws = jnp.exp(jax.random.uniform(jax.random.fold_in(own, axis_at), (blocks,), jnp.float32, low / len(cuts), largest / len(cuts)))
        level = level * jnp.repeat(draws, extent[axis_at] // blocks).reshape([-1 if axis == axis_at else 1 for axis in range(len(extent))])
    return level


def bell_draw(key, dims, scale, bound, shards=(), kind=jnp.bfloat16):
    array = scale * jax.random.normal(key, dims, jnp.float32)
    if shards:
        array = array * steps_of(key, dims, shards, -0.22, 0.18)
    return jnp.clip(array, -bound, bound).astype(kind)


def setup_inputs(seed: int = 0) -> dict:
    key_list = jax.random.split(jax.random.key(seed), 8)
    return {
        "right_side": bell_draw(key_list[0], (NV, ROWS), 1.0, 6.0, ((1, 512),), jnp.float32),
        "start_guess": bell_draw(key_list[1], (NV, ROWS), 1.0, 6.0, ((1, 512),), jnp.float32),
        "fine_matrix": draw_fine_matrix(jax.random.fold_in(key_list[7], 71), 0),
        "fine_columns": draw_fine_columns(jax.random.fold_in(key_list[7], 71), 0),
        "send_lists": touch_ends(jax.random.randint(key_list[4], (DEVICES, 4 * HB), 0, RB), jax.random.fold_in(key_list[4], 1), 0, RB - 1).astype(jnp.int32),
        "aggregates": touch_ends(jax.random.randint(key_list[5], (ROWS,), 0, BS), jax.random.fold_in(key_list[5], 1), 0, BS - 1).astype(jnp.int32),
        "coarse_matrix": draw_coarse_matrix(jax.random.fold_in(key_list[7], 71), 0),
    }


center_value = 1.1
radius_value = 0.9
highest = lax.Precision.HIGHEST


def smooth(operator, inverse, target, start):
    if start is None:
        residual = target
        iterate = jnp.zeros_like(target)
    else:
        residual = target - operator(start)
        iterate = start
    update = inverse * residual / center_value
    iterate = iterate + update
    weight_old = radius_value / center_value
    for sweep in range(2):
        residual = residual - operator(update)
        weight_now = 1.0 / (2.0 * center_value / radius_value - weight_old)
        update = weight_now * weight_old * update + (2.0 * weight_now / radius_value) * inverse * residual
        iterate = iterate + update
        weight_old = weight_now
    return iterate


def neighbours():
    device = jnp.arange(DEVICES, dtype=jnp.int32)
    span_idx = device // N_STREAM
    stream_idx = device % N_STREAM
    near = jnp.stack([device - N_STREAM, device + N_STREAM, device - 1, device + 1], 1)
    valid = jnp.stack([span_idx > 0, span_idx < N_SPAN - 1, stream_idx > 0, stream_idx < N_STREAM - 1], 1)
    near = jnp.clip(near, 0, DEVICES - 1).astype(jnp.int32)
    return near, valid


def fine_operator(vector, fine_matrix, fine_columns, send_lists):
    near, valid = neighbours()
    blocks = vector.reshape(NV, DEVICES, RB, BS)
    lists = send_lists.reshape(DEVICES, 4, HB)
    parts = [blocks]
    for direction in range(4):
        source = near[:, direction]
        chosen = lists[source, direction ^ 1]
        got = blocks[:, source[:, None], chosen]
        parts.append(jnp.where(valid[:, direction][None, :, None, None], got, 0.0))
    extended = jnp.concatenate(parts, axis=2)
    group = 16 if DEVICES % 16 == 0 else 1
    index_all = fine_columns.reshape(DEVICES, RB * NNZB)
    mats = fine_matrix.reshape(DEVICES, RB, NNZB, BS, BS)

    def one_group(number):
        begin = (number * group).astype(jnp.int32)
        sub = lax.dynamic_slice_in_dim(extended, begin, group, axis=1)
        index = lax.dynamic_slice_in_dim(index_all, begin, group, axis=0)
        picked = jnp.take_along_axis(sub, index[None, :, :, None], axis=2)
        picked = picked.reshape(NV, group, RB, NNZB, BS)
        block_mats = lax.dynamic_slice_in_dim(mats, begin, group, axis=0).astype(jnp.float32)
        return jnp.einsum('grkij,vgrkj->gvri', block_mats, picked, precision=highest)

    result = lax.map(one_group, jnp.arange(DEVICES // group, dtype=jnp.int32))
    result = result.reshape(DEVICES, NV, RB, BS).transpose(1, 0, 2, 3)
    return result.reshape(NV, ROWS)


def coarse_operator(vector, coarse_matrix):
    near, valid = neighbours()
    blocks = vector.reshape(NV, DEVICES, BS)
    parts = [blocks]
    for direction in range(4):
        got = blocks[:, near[:, direction]]
        parts.append(jnp.where(valid[:, direction][None, :, None], got, 0.0))
    extended = jnp.stack(parts, axis=2)
    result = jnp.einsum('pkij,vpkj->vpi', coarse_matrix, extended, precision=highest)
    return result.reshape(NV, CROWS)


def reference(right_side, start_guess, fine_matrix, fine_columns, send_lists, aggregates, coarse_matrix):
    fine_inverse = 1.0 / jnp.diagonal(fine_matrix[:, 0], axis1=1, axis2=2).astype(jnp.float32).reshape(ROWS)
    coarse_inverse = 1.0 / jnp.diagonal(coarse_matrix[:, 0], axis1=1, axis2=2).reshape(CROWS)

    def fine_apply(vector):
        return fine_operator(vector, fine_matrix, fine_columns, send_lists)

    def coarse_apply(vector):
        return coarse_operator(vector, coarse_matrix)

    first = smooth(fine_apply, fine_inverse, right_side, start_guess)
    leftover = right_side - fine_apply(first)
    cell_ids = (jnp.arange(ROWS, dtype=jnp.int32) // (RB * BS)) * BS + aggregates.astype(jnp.int32)
    cell_ids = cell_ids.astype(jnp.int32)
    coarse_rhs = jax.ops.segment_sum(leftover.T, cell_ids, num_segments=CROWS).T
    correction = smooth(coarse_apply, coarse_inverse, coarse_rhs, None)
    second = first + correction[:, cell_ids]
    solution = smooth(fine_apply, fine_inverse, right_side, second)
    return (solution, correction)
```

```python
import functools

import jax
import jax.numpy as jnp
from jax import lax
from jax.experimental import pallas as pl
from jax.experimental.pallas import tpu as pltpu
from jax.sharding import PartitionSpec as P

GROUPS = 2

CENTER = 1.1
RADIUS = 0.9
MESH = pl.DeviceIdType.MESH
F32 = jnp.float32
BF16 = jnp.bfloat16
NT = (((1,), (1,)), ((), ()))
NN = (((1,), (0,)), ((), ()))


def coefficients():
    old = RADIUS / CENTER
    pairs = [(0.0, 1.0 / CENTER)]
    for _ in range(2):
        now = 1.0 / (2.0 * CENTER / RADIUS - old)
        pairs.append((now * old, 2.0 * now / RADIUS))
        old = now
    return pairs


def split(value):
    lead = value.astype(BF16).astype(F32)
    return jnp.concatenate([lead, value - lead], axis=0).astype(BF16)


def fold(value):
    half = value.shape[0] // 2
    return value[:half] + value[half:]


def kernel(
    n_span, n_stream, groups, coef,
    cols, lists, x0_hbm, rhs_hbm, mat_hbm, agg_hbm, cmat_hbm,
    sol_hbm, cor_hbm,
    p_ref, r_ref, x_ref, mat, agg, cmat, dinv, cinv, xa, xb, send, recv,
    asend, arecv, own_hot, halo_hot, cweight, csend, crecv, cres, cout,
    mat_t, in_sem, out_sem, ssem, rsem, asem_s, asem_r,
):
    nv, rows = r_ref.shape
    vg = nv // groups
    rb, nnz, bs, _ = mat.shape
    hb = send.shape[3]
    span, stream = lax.axis_index("span"), lax.axis_index("stream")
    has = (span > 0, span < n_span - 1, stream > 0, stream < n_stream - 1)
    near = ((span - 1, stream), (span + 1, stream), (span, stream - 1), (span, stream + 1))
    order = (2, 3, 0, 1)

    loads = [
        pltpu.make_async_copy(x0_hbm, x_ref, in_sem.at[0]),
        pltpu.make_async_copy(agg_hbm, agg, in_sem.at[1]),
        pltpu.make_async_copy(mat_hbm, mat, in_sem.at[2]),
        pltpu.make_async_copy(rhs_hbm, r_ref, in_sem.at[3]),
        pltpu.make_async_copy(cmat_hbm, cmat, in_sem.at[4]),
    ]
    for one in loads:
        one.start()

    barrier = pltpu.get_barrier_semaphore()
    for d in range(4):
        @pl.when(has[d])
        def _():
            pl.semaphore_signal(barrier, inc=1, device_id=near[d], device_id_type=MESH)

    for d in range(4):
        @pl.when(jnp.logical_not(has[d]))
        def _():
            recv[:, :, d] = jnp.zeros(recv.shape[:2] + recv.shape[3:], F32)
            crecv[:, :, d] = jnp.zeros(crecv.shape[:2] + crecv.shape[3:], F32)
            arecv[d] = jnp.zeros(arecv.shape[1:], jnp.int32)

    peers = sum(one.astype(jnp.int32) for one in has)
    pl.semaphore_wait(barrier, peers)

    def fine_copy(n, g, d):
        return pltpu.make_async_remote_copy(
            src_ref=send.at[n, g, d], dst_ref=recv.at[n, g, d ^ 1],
            send_sem=ssem.at[n, g, d], recv_sem=rsem.at[n, g, d ^ 1],
            device_id=near[d], device_id_type=MESH)

    def coarse_copy(m, g, d):
        return pltpu.make_async_remote_copy(
            src_ref=csend.at[m, g], dst_ref=crecv.at[m, g, d ^ 1],
            send_sem=ssem.at[6 + m, g, d], recv_sem=rsem.at[6 + m, g, d ^ 1],
            device_id=near[d], device_id_type=MESH)

    def agg_copy(d):
        return pltpu.make_async_remote_copy(
            src_ref=asend.at[d], dst_ref=arecv.at[d ^ 1],
            send_sem=asem_s.at[d], recv_sem=asem_r.at[d ^ 1],
            device_id=near[d], device_id_type=MESH)

    def block_of(g, b):
        return (pl.ds(pl.multiple_of(g * vg, vg), vg), pl.ds(b * bs, bs))

    def send_fine(n, g):
        for d in order:
            @pl.when(has[d])
            def _():
                for h in range(hb):
                    send[n, g, d, h] = p_ref[g, lists[0, d * hb + h]]
                fine_copy(n, g, d).start()

    def send_coarse(m, g, value):
        csend[m, g] = value
        for d in order:
            @pl.when(has[d])
            def _():
                coarse_copy(m, g, d).start()

    def arrived(copy_of, first, g):
        for d in order:
            @pl.when(has[d])
            def _():
                copy_of(first, g, d ^ 1).wait_recv()

    def loop(body):
        lax.fori_loop(0, groups, lambda g, _: (body(g), 0)[1], 0)

    loads[0].wait()

    def start(g):
        for b in range(rb):
            value = x_ref[block_of(g, b)]
            p_ref[g, b] = value
            xa[g, b] = split(value)
        send_fine(0, g)

    loop(start)
    loads[1].wait()
    for d in range(4):
        for h in range(hb):
            asend[d, h] = agg[lists[0, d * hb + h]]
    for d in range(4):
        @pl.when(has[d])
        def _():
            agg_copy(d).start()

    row_id = lax.broadcasted_iota(jnp.int32, (bs, bs), 0)
    lane_id = lax.broadcasted_iota(jnp.int32, (bs, bs), 1)
    eye = row_id == lane_id
    for b in range(rb):
        own_hot[:, pl.ds(b * bs, bs)] = (
            jnp.broadcast_to(agg[b], (bs, bs)) == row_id).astype(F32).astype(BF16)
    loads[2].wait()
    for b in range(rb):
        diag = jnp.sum(jnp.where(eye, mat[b, 0].astype(F32), 0.0), axis=0, keepdims=True)
        dinv[pl.ds(b, 1), :] = 1.0 / diag
        for k in range(nnz):
            mat_t[b, pl.ds(k * bs, bs), :] = mat[b, k].T
    loads[4].wait()
    cinv[...] = jnp.broadcast_to(
        1.0 / jnp.sum(jnp.where(eye, cmat[0, 0], 0.0), axis=0, keepdims=True), cinv.shape)
    for k in range(5):
        cweight[k] = split(cmat[0, k])
    for d in range(4):
        @pl.when(has[d])
        def _():
            agg_copy(d ^ 1).wait_recv()
        for h in range(hb):
            halo_hot[d, :, pl.ds(h * bs, bs)] = (
                jnp.broadcast_to(arecv[d, h], (bs, bs)) == row_id
            ).astype(F32).astype(BF16)
    loads[3].wait()

    def take_halo(n, g, x):
        arrived(fine_copy, n, g)
        for d in range(4):
            for h in range(hb):
                x[g, rb + d * hb + h] = split(recv[n, g, d, h])

    def apply(g, x, nxt, alpha, beta, kind):
        for b in range(rb):
            left = jnp.concatenate(
                [x[g, b]] + [x[g, cols[k, b]] for k in range(1, nnz)], axis=1)
            prod = fold(lax.dot_general(left, mat_t[b], NN, preferred_element_type=F32))
            at = block_of(g, b)
            y = p_ref[g, b]
            res = r_ref[at] - prod
            step = beta * (dinv[pl.ds(b, 1), :] * res)
            if alpha:
                step = alpha * y + step
            if kind == "last":
                x_ref[at] = x_ref[at] + y + step
                continue
            if kind != "first":
                x_ref[at] = x_ref[at] + y
            r_ref[at] = res
            if kind != "leftover":
                p_ref[g, b] = step
                nxt[g, b] = split(step)

    def sweep(n, x, nxt, kind):
        def one(g):
            take_halo(n, g, x)
            apply(g, x, nxt, *coef[n % 3], kind)
            send_fine(n + 1, g)

        loop(one)

    sweep(0, xa, xb, "first")
    sweep(1, xb, xa, "")
    sweep(2, xa, xb, "")

    def restrict(g):
        take_halo(3, g, xb)
        apply(g, xb, None, *coef[0], "leftover")
        left = split(r_ref[pl.ds(pl.multiple_of(g * vg, vg), vg), :])
        res = fold(lax.dot_general(left, own_hot[...], NT, preferred_element_type=F32))
        cres[g] = res
        start = cinv[pl.ds(0, 1), :] * res * coef[0][1]
        cout[g] = start
        send_coarse(0, g, start)

    loop(restrict)

    def coarse_sweep(m):
        def one(g):
            arrived(coarse_copy, m, g)
            old = csend[m, g]
            left = jnp.concatenate(
                [split(old)] + [split(crecv[m, g, d]) for d in range(4)], axis=1)
            right = jnp.concatenate([cweight[k] for k in range(5)], axis=1)
            full = fold(lax.dot_general(left, right, NT, preferred_element_type=F32))
            res = cres[g] - (full[:, :bs] + full[:, bs:])
            cres[g] = res
            alpha, beta = coef[m + 1]
            step = alpha * old + beta * (cinv[pl.ds(0, 1), :] * res)
            cout[g] = cout[g] + step
            send_coarse(m + 1, g, step)

        loop(one)

    coarse_sweep(0)
    coarse_sweep(1)
    cor_copy = pltpu.make_async_copy(cout, cor_hbm, out_sem.at[groups])
    cor_copy.start()

    def prolong(g):
        arrived(coarse_copy, 2, g)
        left = split(cout[g])
        for b in range(rb):
            part = lax.dot_general(
                left, own_hot[:, pl.ds(b * bs, bs)], NN, preferred_element_type=F32)
            value = fold(part)
            p_ref[g, b] = value
            xa[g, b] = split(value)
        for d in range(4):
            other = crecv[0, g, d] + crecv[1, g, d] + crecv[2, g, d]
            left = split(other)
            for h in range(hb):
                got = lax.dot_general(
                    left, halo_hot[d, :, pl.ds(h * bs, bs)], NN, preferred_element_type=F32)
                xa[g, rb + d * hb + h] = split(fold(got))

    def coarse_back(g):
        prolong(g)
        apply(g, xa, xb, *coef[0], "")
        send_fine(4, g)

    loop(coarse_back)
    sweep(4, xb, xa, "")

    def out_copy(g):
        at = pl.ds(pl.multiple_of(g * vg, vg), vg)
        return pltpu.make_async_copy(x_ref.at[at], sol_hbm.at[at], out_sem.at[g])

    def finish(g):
        take_halo(5, g, xa)
        apply(g, xa, None, *coef[2], "last")
        out_copy(g).start()

    loop(finish)

    for d in range(4):
        @pl.when(has[d])
        def _():
            def drain(g):
                for n in range(6):
                    fine_copy(n, g, d).wait_send()
                for m in range(3):
                    coarse_copy(m, g, d).wait_send()

            loop(drain)
            agg_copy(d).wait_send()
    loop(lambda g: out_copy(g).wait())
    cor_copy.wait()


def local(
    right_side, start_guess, fine_matrix, fine_columns, send_lists, aggregates, coarse_matrix,
    n_span, n_stream,
):
    nv, rows = right_side.shape
    rb, nnz, bs, _ = fine_matrix.shape
    hb = send_lists.shape[1] // 4
    groups = GROUPS
    vg = nv // groups
    any_spec = pl.BlockSpec(memory_space=pl.ANY)
    smem = pl.BlockSpec(memory_space=pltpu.SMEM)
    dma = pltpu.SemaphoreType.DMA
    solution, correction = pl.pallas_call(
        functools.partial(kernel, n_span, n_stream, groups, coefficients()),
        out_shape=(
            jax.ShapeDtypeStruct((nv, rows), F32),
            jax.ShapeDtypeStruct((groups, vg, bs), F32),
        ),
        in_specs=[smem, smem] + [any_spec] * 5,
        out_specs=(any_spec, any_spec),
        scratch_shapes=[
            pltpu.VMEM((groups, rb, vg, bs), F32),
            pltpu.VMEM((nv, rows), F32),
            pltpu.VMEM((nv, rows), F32),
            pltpu.VMEM((rb, nnz, bs, bs), BF16),
            pltpu.VMEM((rb, 1, bs), jnp.int32),
            pltpu.VMEM((1, 5, bs, bs), F32),
            pltpu.VMEM((rb, bs), F32),
            pltpu.VMEM((8, bs), F32),
            pltpu.VMEM((groups, rb + 4 * hb, 2 * vg, bs), BF16),
            pltpu.VMEM((groups, rb + 4 * hb, 2 * vg, bs), BF16),
            pltpu.VMEM((6, groups, 4, hb, vg, bs), F32),
            pltpu.VMEM((6, groups, 4, hb, vg, bs), F32),
            pltpu.VMEM((4, hb, 1, bs), jnp.int32),
            pltpu.VMEM((4, hb, 1, bs), jnp.int32),
            pltpu.VMEM((bs, rows), BF16),
            pltpu.VMEM((4, bs, hb * bs), BF16),
            pltpu.VMEM((5, 2 * bs, bs), BF16),
            pltpu.VMEM((3, groups, vg, bs), F32),
            pltpu.VMEM((3, groups, 4, vg, bs), F32),
            pltpu.VMEM((groups, vg, bs), F32),
            pltpu.VMEM((groups, vg, bs), F32),
            pltpu.VMEM((rb, nnz * bs, bs), BF16),
            dma((5,)),
            dma((groups + 1,)),
            dma((9, groups, 4)),
            dma((9, groups, 4)),
            dma((4,)),
            dma((4,)),
        ],
        compiler_params=pltpu.CompilerParams(
            collective_id=0, has_side_effects=True, vmem_limit_bytes=62 * 1024 * 1024),
        name="cycle",
    )(
        fine_columns.T, send_lists, start_guess, right_side, fine_matrix,
        aggregates.reshape(rb, 1, bs), coarse_matrix,
    )
    return solution, correction.reshape(nv, bs)


def solution(mesh):
    placed = (
        P(None, ("span", "stream")),
        P(None, ("span", "stream")),
        P(("span", "stream"), None, None, None),
        P(("span", "stream"), None),
        P(("span", "stream"), None),
        P(("span", "stream")),
        P(("span", "stream"), None, None, None),
    )
    return jax.shard_map(
        functools.partial(local, n_span=mesh.shape["span"], n_stream=mesh.shape["stream"]),
        mesh=mesh,
        in_specs=placed,
        out_specs=(P(None, ("span", "stream")), P(None, ("span", "stream"))),
        check_vma=False,
    )
```

```python
import functools

import jax
import jax.numpy as jnp
from jax import lax
from jax.experimental import pallas as pl
from jax.experimental.pallas import tpu as pltpu
from jax.sharding import PartitionSpec as P

GROUPS = 2
COLUMN = 8

CENTER = 1.1
RADIUS = 0.9
MESH = pl.DeviceIdType.MESH
F32 = jnp.float32
BF16 = jnp.bfloat16
NT = (((1,), (1,)), ((), ()))
NN = (((1,), (0,)), ((), ()))


def coefficients():
    old = RADIUS / CENTER
    pairs = [(0.0, 1.0 / CENTER)]
    for _ in range(2):
        now = 1.0 / (2.0 * CENTER / RADIUS - old)
        pairs.append((now * old, 2.0 * now / RADIUS))
        old = now
    return pairs


def split(value):
    lead = value.astype(BF16).astype(F32)
    return jnp.concatenate([lead, value - lead], axis=0).astype(BF16)


def fold(value):
    half = value.shape[0] // 2
    return value[:half] + value[half:]


def kernel(
    n_span, n_stream, groups, coef,
    cols, lists, x0_hbm, rhs_hbm, mat_hbm, agg_hbm, cmat_hbm,
    sol_hbm, cor_hbm,
    pa, pb, ra, rb_, rhs, x_ref, mat, agg, cmat, dinv, cinv, xa, xb, send, recv,
    asend, arecv, own_hot, halo_hot, cweight, csend, crecv, cres, cout,
    mat_t, in_sem, out_sem, ssem, rsem, asem_s, asem_r,
):
    nv, rows = rhs.shape
    vg = nv // groups
    rb, nnz, bs, _ = mat.shape
    hb = send.shape[3]
    span, stream = lax.axis_index("span"), lax.axis_index("stream")
    has = (span > 0, span < n_span - 1, stream > 0, stream < n_stream - 1)
    near = ((span - 1, stream), (span + 1, stream), (span, stream - 1), (span, stream + 1))
    order = (2, 3, 0, 1)

    loads = [
        pltpu.make_async_copy(x0_hbm, x_ref, in_sem.at[0]),
        pltpu.make_async_copy(agg_hbm, agg, in_sem.at[1]),
        pltpu.make_async_copy(mat_hbm, mat, in_sem.at[2]),
        pltpu.make_async_copy(rhs_hbm, rhs, in_sem.at[3]),
        pltpu.make_async_copy(cmat_hbm, cmat, in_sem.at[4]),
    ]
    for one in loads:
        one.start()

    barrier = pltpu.get_barrier_semaphore()
    for d in range(4):
        @pl.when(has[d])
        def _():
            pl.semaphore_signal(barrier, inc=1, device_id=near[d], device_id_type=MESH)

    for d in range(4):
        @pl.when(jnp.logical_not(has[d]))
        def _():
            recv[:, :, d] = jnp.zeros(recv.shape[:2] + recv.shape[3:], F32)
            crecv[:, :, d] = jnp.zeros(crecv.shape[:2] + crecv.shape[3:], F32)
            arecv[d] = jnp.zeros(arecv.shape[1:], jnp.int32)

    peers = sum(one.astype(jnp.int32) for one in has)
    pl.semaphore_wait(barrier, peers)

    def fine_copy(n, g, d):
        return pltpu.make_async_remote_copy(
            src_ref=send.at[n, g, d], dst_ref=recv.at[n, g, d ^ 1],
            send_sem=ssem.at[n, g, d], recv_sem=rsem.at[n, g, d ^ 1],
            device_id=near[d], device_id_type=MESH)

    def coarse_copy(m, g, d):
        return pltpu.make_async_remote_copy(
            src_ref=csend.at[m, g], dst_ref=crecv.at[m, g, d ^ 1],
            send_sem=ssem.at[6 + m, g, d], recv_sem=rsem.at[6 + m, g, d ^ 1],
            device_id=near[d], device_id_type=MESH)

    def agg_copy(d):
        return pltpu.make_async_remote_copy(
            src_ref=asend.at[d], dst_ref=arecv.at[d ^ 1],
            send_sem=asem_s.at[d], recv_sem=asem_r.at[d ^ 1],
            device_id=near[d], device_id_type=MESH)

    def block_of(g, b):
        return (pl.ds(pl.multiple_of(g * vg, vg), vg), pl.ds(b * bs, bs))

    def send_fine(n, g, p, dirs):
        for d in dirs:
            @pl.when(has[d])
            def _():
                for h in range(hb):
                    send[n, g, d, h] = p[g, lists[0, d * hb + h]]
                fine_copy(n, g, d).start()

    def send_coarse(m, g, value):
        csend[m, g] = value
        for d in order:
            @pl.when(has[d])
            def _():
                coarse_copy(m, g, d).start()

    def arrived(copy_of, first, g):
        for d in order:
            @pl.when(has[d])
            def _():
                copy_of(first, g, d ^ 1).wait_recv()

    def loop(body):
        lax.fori_loop(0, groups, lambda g, _: (body(g), 0)[1], 0)

    loads[0].wait()

    def start(g):
        for b in range(rb):
            pa[g, b] = x_ref[block_of(g, b)]
        send_fine(0, g, pa, order)

    loop(start)
    loads[1].wait()
    for d in range(4):
        for h in range(hb):
            asend[d, h] = agg[lists[0, d * hb + h]]
    for d in range(4):
        @pl.when(has[d])
        def _():
            agg_copy(d).start()

    def split_start(g):
        for b in range(rb):
            xa[g, b] = split(x_ref[block_of(g, b)])

    loop(split_start)
    row_id = lax.broadcasted_iota(jnp.int32, (bs, bs), 0)
    lane_id = lax.broadcasted_iota(jnp.int32, (bs, bs), 1)
    eye = row_id == lane_id
    for b in range(rb):
        own_hot[:, pl.ds(b * bs, bs)] = (
            jnp.broadcast_to(agg[b], (bs, bs)) == row_id).astype(F32).astype(BF16)
    loads[2].wait()
    for b in range(rb):
        diag = jnp.sum(jnp.where(eye, mat[b, 0].astype(F32), 0.0), axis=0, keepdims=True)
        dinv[b] = 1.0 / diag
        for k in range(nnz):
            mat_t[b, pl.ds(k * bs, bs), :] = mat[b, k].T
    loads[4].wait()
    cinv[...] = jnp.broadcast_to(
        1.0 / jnp.sum(jnp.where(eye, cmat[0, 0], 0.0), axis=0, keepdims=True), cinv.shape)
    for k in range(5):
        cweight[k] = split(cmat[0, k])
    for d in range(4):
        @pl.when(has[d])
        def _():
            agg_copy(d ^ 1).wait_recv()
        for h in range(hb):
            halo_hot[d, :, pl.ds(h * bs, bs)] = (
                jnp.broadcast_to(arecv[d, h], (bs, bs)) == row_id
            ).astype(F32).astype(BF16)
    loads[3].wait()

    def block_rhs(g):
        for b in range(rb):
            ra[g, b] = rhs[block_of(g, b)]

    loop(block_rhs)

    def take_halo(n, g, x):
        arrived(fine_copy, n, g)
        for d in range(4):
            for h in range(hb):
                x[g, rb + d * hb + h] = split(recv[n, g, d, h])

    def product(g, b, x):
        left = jnp.concatenate([x[g, b]] + [x[g, cols[k, b]] for k in range(1, nnz)], axis=1)
        return fold(lax.dot_general(left, mat_t[b], NN, preferred_element_type=F32))

    def update(g, b, res, p, alpha, beta):
        step = beta * (dinv[b] * res)
        return alpha * p[g, b] + step if alpha else step

    def ahead(n, g, x, p, r, alpha, beta):
        for d in (far, 5 - far):
            for h in range(hb):
                b = lists[0, d * hb + h]
                send[n, g, d, h] = update(g, b, r[g, b] - product(g, b, x), p, alpha, beta)

            @pl.when(jnp.where(d == 2, stream > 0, stream < n_stream - 1))
            def _():
                pltpu.make_async_remote_copy(
                    src_ref=send.at[n, g, d], dst_ref=recv.at[n, g, 5 - d],
                    send_sem=ssem.at[n, g, d], recv_sem=rsem.at[n, g, 5 - d],
                    device_id=(span, stream + 2 * d - 5), device_id_type=MESH).start()

    def apply(g, now, nxt, alpha, beta, kind):
        x, p, r = now
        for b in range(rb):
            res = r[g, b] - product(g, b, x)
            at = block_of(g, b)
            if kind == "last":
                x_ref[at] = x_ref[at] + p[g, b] + update(g, b, res, p, alpha, beta)
                continue
            if kind != "first":
                x_ref[at] = x_ref[at] + p[g, b]
            nxt[2][g, b] = res
            if kind != "leftover":
                step = update(g, b, res, p, alpha, beta)
                nxt[1][g, b] = step
                nxt[0][g, b] = split(step)

    def advance(n, g, now, nxt, alpha, beta, kind):
        ahead(n, g, *now, alpha, beta)
        apply(g, now, nxt, alpha, beta, kind)
        send_fine(n, g, nxt[1], (0, 1))

    even, odd = (xa, pa, ra), (xb, pb, rb_)
    far = jnp.where(stream % COLUMN == 0, 2, 3)

    def sweep(n, now, nxt, kind):
        def one(g):
            take_halo(n, g, now[0])
            advance(n + 1, g, now, nxt, *coef[n % 3], kind)

        loop(one)

    sweep(0, even, odd, "first")
    sweep(1, odd, even, "")
    sweep(2, even, odd, "")

    def restrict(g):
        take_halo(3, g, xb)
        apply(g, odd, even, *coef[0], "leftover")
        left = split(jnp.concatenate([ra[g, b] for b in range(rb)], axis=1))
        res = fold(lax.dot_general(left, own_hot[...], NT, preferred_element_type=F32))
        cres[g] = res
        start = cinv[pl.ds(0, 1), :] * res * coef[0][1]
        cout[g] = start
        send_coarse(0, g, start)

    loop(restrict)

    def coarse_sweep(m):
        def one(g):
            arrived(coarse_copy, m, g)
            old = csend[m, g]
            left = jnp.concatenate(
                [split(old)] + [split(crecv[m, g, d]) for d in range(4)], axis=1)
            right = jnp.concatenate([cweight[k] for k in range(5)], axis=1)
            full = fold(lax.dot_general(left, right, NT, preferred_element_type=F32))
            res = cres[g] - (full[:, :bs] + full[:, bs:])
            cres[g] = res
            alpha, beta = coef[m + 1]
            step = alpha * old + beta * (cinv[pl.ds(0, 1), :] * res)
            cout[g] = cout[g] + step
            send_coarse(m + 1, g, step)

        loop(one)

    coarse_sweep(0)
    coarse_sweep(1)
    cor_copy = pltpu.make_async_copy(cout, cor_hbm, out_sem.at[groups])
    cor_copy.start()

    def prolong_own(g):
        left = split(cout[g])
        for b in range(rb):
            part = lax.dot_general(
                left, own_hot[:, pl.ds(b * bs, bs)], NN, preferred_element_type=F32)
            value = fold(part)
            pa[g, b] = value
            xa[g, b] = split(value)

    loop(prolong_own)

    def prolong(g):
        arrived(coarse_copy, 2, g)
        for d in range(4):
            other = crecv[0, g, d] + crecv[1, g, d] + crecv[2, g, d]
            left = split(other)
            for h in range(hb):
                got = lax.dot_general(
                    left, halo_hot[d, :, pl.ds(h * bs, bs)], NN, preferred_element_type=F32)
                xa[g, rb + d * hb + h] = split(fold(got))

    def coarse_back(g):
        prolong(g)
        advance(4, g, even, odd, *coef[0], "")

    loop(coarse_back)
    sweep(4, odd, even, "")

    for d in range(4):
        @pl.when(has[d])
        def _():
            def drain(g):
                for n in range(6):
                    fine_copy(n, g, d).wait_send()
                for m in range(3):
                    coarse_copy(m, g, d).wait_send()

            loop(drain)
            agg_copy(d).wait_send()
    def out_copy(g):
        at = pl.ds(pl.multiple_of(g * vg, vg), vg)
        return pltpu.make_async_copy(x_ref.at[at], sol_hbm.at[at], out_sem.at[g])

    def finish(g):
        take_halo(5, g, xa)
        apply(g, even, None, *coef[2], "last")
        out_copy(g).start()

    loop(finish)

    loop(lambda g: out_copy(g).wait())
    cor_copy.wait()


def carry(sol_in, cor_in, sol_out, cor_out, sem):
    copies = [
        pltpu.make_async_copy(cor_in, cor_out, sem.at[0]),
        pltpu.make_async_copy(sol_in, sol_out, sem.at[1]),
    ]
    for one in copies:
        one.start()
    for one in copies:
        one.wait()


def local(
    right_side, start_guess, fine_matrix, fine_columns, send_lists, aggregates, coarse_matrix,
    n_span, n_stream,
):
    nv, rows = right_side.shape
    rb, nnz, bs, _ = fine_matrix.shape
    hb = send_lists.shape[1] // 4
    groups = GROUPS
    vg = nv // groups
    any_spec = pl.BlockSpec(memory_space=pl.ANY)
    hbm = functools.partial(pltpu.with_memory_space_constraint, memory_space=pltpu.HBM)
    smem = pl.BlockSpec(memory_space=pltpu.SMEM)
    dma = pltpu.SemaphoreType.DMA
    solution, correction = pl.pallas_call(
        functools.partial(kernel, n_span, n_stream, groups, coefficients()),
        out_shape=(
            jax.ShapeDtypeStruct((nv, rows), F32),
            jax.ShapeDtypeStruct((groups, vg, bs), F32),
        ),
        in_specs=[smem, smem] + [any_spec] * 5,
        out_specs=(any_spec, any_spec),
        scratch_shapes=[
            pltpu.VMEM((groups, rb, vg, bs), F32),
            pltpu.VMEM((groups, rb, vg, bs), F32),
            pltpu.VMEM((groups, rb, vg, bs), F32),
            pltpu.VMEM((groups, rb, vg, bs), F32),
            pltpu.VMEM((nv, rows), F32),
            pltpu.VMEM((nv, rows), F32),
            pltpu.VMEM((rb, nnz, bs, bs), BF16),
            pltpu.VMEM((rb, 1, bs), jnp.int32),
            pltpu.VMEM((1, 5, bs, bs), F32),
            pltpu.VMEM((rb, 1, bs), F32),
            pltpu.VMEM((8, bs), F32),
            pltpu.VMEM((groups, rb + 4 * hb, 2 * vg, bs), BF16),
            pltpu.VMEM((groups, rb + 4 * hb, 2 * vg, bs), BF16),
            pltpu.VMEM((6, groups, 4, hb, vg, bs), F32),
            pltpu.VMEM((6, groups, 4, hb, vg, bs), F32),
            pltpu.VMEM((4, hb, 1, bs), jnp.int32),
            pltpu.VMEM((4, hb, 1, bs), jnp.int32),
            pltpu.VMEM((bs, rows), BF16),
            pltpu.VMEM((4, bs, hb * bs), BF16),
            pltpu.VMEM((5, 2 * bs, bs), BF16),
            pltpu.VMEM((3, groups, vg, bs), F32),
            pltpu.VMEM((3, groups, 4, vg, bs), F32),
            pltpu.VMEM((groups, vg, bs), F32),
            pltpu.VMEM((groups, vg, bs), F32),
            pltpu.VMEM((rb, nnz * bs, bs), BF16),
            dma((5,)),
            dma((groups + 1,)),
            dma((9, groups, 4)),
            dma((9, groups, 4)),
            dma((4,)),
            dma((4,)),
        ],
        compiler_params=pltpu.CompilerParams(
            collective_id=0, has_side_effects=True, vmem_limit_bytes=28 * 1024 * 1024),
        name="cycle",
    )(
        hbm(fine_columns.T), hbm(send_lists), hbm(start_guess), hbm(right_side), hbm(fine_matrix),
        hbm(aggregates.reshape(rb, 1, bs)), hbm(coarse_matrix),
    )
    return pl.pallas_call(
        carry,
        out_shape=(
            jax.ShapeDtypeStruct((nv, rows), F32), jax.ShapeDtypeStruct((nv, bs), F32)),
        in_specs=[any_spec, any_spec],
        out_specs=(any_spec, any_spec),
        scratch_shapes=[dma((2,))],
        compiler_params=pltpu.CompilerParams(vmem_limit_bytes=8 * 1024 * 1024),
        name="carry",
    )(solution, correction.reshape(nv, bs))


def solution(mesh):
    placed = (
        P(None, ("span", "stream")),
        P(None, ("span", "stream")),
        P(("span", "stream"), None, None, None),
        P(("span", "stream"), None),
        P(("span", "stream"), None),
        P(("span", "stream")),
        P(("span", "stream"), None, None, None),
    )
    return jax.shard_map(
        functools.partial(local, n_span=mesh.shape["span"], n_stream=mesh.shape["stream"]),
        mesh=mesh,
        in_specs=placed,
        out_specs=(P(None, ("span", "stream")), P(None, ("span", "stream"))),
        check_vma=False,
    )
```

```python
import functools

import jax
import jax.numpy as jnp
from jax import lax
from jax.experimental import pallas as pl
from jax.experimental.pallas import tpu as pltpu
from jax.sharding import PartitionSpec as P

GROUPS = 2
COLUMN = 8

CENTER = 1.1
RADIUS = 0.9
MESH = pl.DeviceIdType.MESH
F32 = jnp.float32
BF16 = jnp.bfloat16
NT = (((1,), (1,)), ((), ()))
NN = (((1,), (0,)), ((), ()))


def coefficients():
    old = RADIUS / CENTER
    pairs = [(0.0, 1.0 / CENTER)]
    for _ in range(2):
        now = 1.0 / (2.0 * CENTER / RADIUS - old)
        pairs.append((now * old, 2.0 * now / RADIUS))
        old = now
    return pairs


def split(value):
    lead = value.astype(BF16).astype(F32)
    return jnp.concatenate([lead, value - lead], axis=0).astype(BF16)


def fold(value):
    half = value.shape[0] // 2
    return value[:half] + value[half:]


def kernel(
    n_span, n_stream, groups, coef,
    cols, lists, x0_hbm, rhs_hbm, mat_hbm, agg_hbm, cmat_hbm,
    sol_hbm, cor_hbm,
    pa, pb, ra, rb_, rhs, x_ref, mat, agg, cmat, dinv, cinv, xa, xb, send, recv,
    asend, arecv, own_hot, halo_hot, cweight, csend, crecv, cres, cout,
    mat_t, in_sem, out_sem, ssem, rsem, asem_s, asem_r,
):
    nv, rows = rhs.shape
    vg = nv // groups
    rb, nnz, bs, _ = mat.shape
    hb = send.shape[3]
    span, stream = lax.axis_index("span"), lax.axis_index("stream")
    has = (span > 0, span < n_span - 1, stream > 0, stream < n_stream - 1)
    near = ((span - 1, stream), (span + 1, stream), (span, stream - 1), (span, stream + 1))
    order = (2, 3, 0, 1)

    loads = [
        pltpu.make_async_copy(x0_hbm, x_ref, in_sem.at[0]),
        pltpu.make_async_copy(agg_hbm, agg, in_sem.at[1]),
        pltpu.make_async_copy(mat_hbm, mat, in_sem.at[2]),
        pltpu.make_async_copy(rhs_hbm, rhs, in_sem.at[3]),
        pltpu.make_async_copy(cmat_hbm, cmat, in_sem.at[4]),
    ]
    for one in loads:
        one.start()

    barrier = pltpu.get_barrier_semaphore()
    for d in range(4):
        @pl.when(has[d])
        def _():
            pl.semaphore_signal(barrier, inc=1, device_id=near[d], device_id_type=MESH)

    for d in range(4):
        @pl.when(jnp.logical_not(has[d]))
        def _():
            recv[:, :, d] = jnp.zeros(recv.shape[:2] + recv.shape[3:], F32)
            crecv[:, :, d] = jnp.zeros(crecv.shape[:2] + crecv.shape[3:], F32)
            arecv[d] = jnp.zeros(arecv.shape[1:], jnp.int32)

    peers = sum(one.astype(jnp.int32) for one in has)
    pl.semaphore_wait(barrier, peers)

    def fine_copy(n, g, d):
        return pltpu.make_async_remote_copy(
            src_ref=send.at[n, g, d], dst_ref=recv.at[n, g, d ^ 1],
            send_sem=ssem.at[n, g, d], recv_sem=rsem.at[n, g, d ^ 1],
            device_id=near[d], device_id_type=MESH)

    def coarse_copy(m, g, d):
        return pltpu.make_async_remote_copy(
            src_ref=csend.at[m, g], dst_ref=crecv.at[m, g, d ^ 1],
            send_sem=ssem.at[6 + m, g, d], recv_sem=rsem.at[6 + m, g, d ^ 1],
            device_id=near[d], device_id_type=MESH)

    def agg_copy(d):
        return pltpu.make_async_remote_copy(
            src_ref=asend.at[d], dst_ref=arecv.at[d ^ 1],
            send_sem=asem_s.at[d], recv_sem=asem_r.at[d ^ 1],
            device_id=near[d], device_id_type=MESH)

    def block_of(g, b):
        return (pl.ds(pl.multiple_of(g * vg, vg), vg), pl.ds(b * bs, bs))

    def send_fine(n, g, p, dirs):
        for d in dirs:
            @pl.when(has[d])
            def _():
                for h in range(hb):
                    send[n, g, d, h] = p[g, lists[0, d * hb + h]]
                fine_copy(n, g, d).start()

    def send_coarse(m, g, value):
        csend[m, g] = value
        for d in order:
            @pl.when(has[d])
            def _():
                coarse_copy(m, g, d).start()

    def arrived(copy_of, first, g):
        for d in order:
            @pl.when(has[d])
            def _():
                copy_of(first, g, d ^ 1).wait_recv()

    def loop(body):
        lax.fori_loop(0, groups, lambda g, _: (body(g), 0)[1], 0)

    loads[0].wait()

    def start(g):
        for b in range(rb):
            pa[g, b] = x_ref[block_of(g, b)]
        send_fine(0, g, pa, order)

    loop(start)
    loads[1].wait()
    for d in range(4):
        for h in range(hb):
            asend[d, h] = agg[lists[0, d * hb + h]]
    for d in range(4):
        @pl.when(has[d])
        def _():
            agg_copy(d).start()

    def split_start(g):
        for b in range(rb):
            xa[g, b] = split(x_ref[block_of(g, b)])

    loop(split_start)
    row_id = lax.broadcasted_iota(jnp.int32, (bs, bs), 0)
    lane_id = lax.broadcasted_iota(jnp.int32, (bs, bs), 1)
    eye = row_id == lane_id
    for b in range(rb):
        own_hot[:, pl.ds(b * bs, bs)] = (
            jnp.broadcast_to(agg[b], (bs, bs)) == row_id).astype(F32).astype(BF16)
    loads[2].wait()
    for b in range(rb):
        diag = jnp.sum(jnp.where(eye, mat[b, 0].astype(F32), 0.0), axis=0, keepdims=True)
        dinv[b] = 1.0 / diag
        for k in range(nnz):
            mat_t[b, pl.ds(k * bs, bs), :] = mat[b, k].T
    loads[4].wait()
    cinv[...] = jnp.broadcast_to(
        1.0 / jnp.sum(jnp.where(eye, cmat[0, 0], 0.0), axis=0, keepdims=True), cinv.shape)
    for k in range(5):
        cweight[k] = split(cmat[0, k])
    for d in range(4):
        @pl.when(has[d])
        def _():
            agg_copy(d ^ 1).wait_recv()
        for h in range(hb):
            halo_hot[d, :, pl.ds(h * bs, bs)] = (
                jnp.broadcast_to(arecv[d, h], (bs, bs)) == row_id
            ).astype(F32).astype(BF16)
    loads[3].wait()

    def block_rhs(g):
        for b in range(rb):
            ra[g, b] = rhs[block_of(g, b)]

    loop(block_rhs)

    def take_halo(n, g, x):
        arrived(fine_copy, n, g)
        for d in range(4):
            for h in range(hb):
                x[g, rb + d * hb + h] = split(recv[n, g, d, h])

    def product(g, b, x):
        left = jnp.concatenate([x[g, b]] + [x[g, cols[k, b]] for k in range(1, nnz)], axis=1)
        return fold(lax.dot_general(left, mat_t[b], NN, preferred_element_type=F32))

    def update(g, b, res, p, alpha, beta):
        step = beta * (dinv[b] * res)
        return alpha * p[g, b] + step if alpha else step

    def ahead(n, g, x, p, r, alpha, beta):
        for h in range(hb):
            b = lists[0, far * hb + h]
            send[n, g, far, h] = update(g, b, r[g, b] - product(g, b, x), p, alpha, beta)
        pltpu.make_async_remote_copy(
            src_ref=send.at[n, g, far], dst_ref=recv.at[n, g, 5 - far],
            send_sem=ssem.at[n, g, far], recv_sem=rsem.at[n, g, 5 - far],
            device_id=(span, stream + 2 * far - 5), device_id_type=MESH).start()

    def apply(g, now, nxt, alpha, beta, kind):
        x, p, r = now
        for b in range(rb):
            res = r[g, b] - product(g, b, x)
            at = block_of(g, b)
            if kind == "last":
                x_ref[at] = x_ref[at] + p[g, b] + update(g, b, res, p, alpha, beta)
                continue
            if kind != "first":
                x_ref[at] = x_ref[at] + p[g, b]
            nxt[2][g, b] = res
            if kind != "leftover":
                step = update(g, b, res, p, alpha, beta)
                nxt[1][g, b] = step
                nxt[0][g, b] = split(step)

    def advance(n, g, now, nxt, alpha, beta, kind):
        @pl.when(edge)
        def _():
            ahead(n, g, *now, alpha, beta)

        apply(g, now, nxt, alpha, beta, kind)
        for d in order:
            @pl.when(jnp.logical_and(has[d], jnp.logical_not(jnp.logical_and(edge, far == d))))
            def _():
                for h in range(hb):
                    send[n, g, d, h] = nxt[1][g, lists[0, d * hb + h]]
                fine_copy(n, g, d).start()

    even, odd = (xa, pa, ra), (xb, pb, rb_)
    low = stream % COLUMN == 0
    far = jnp.where(low, 2, 3)
    edge = jnp.logical_or(
        jnp.logical_and(low, has[2]), jnp.logical_and(stream % COLUMN == COLUMN - 1, has[3]))

    def sweep(n, now, nxt, kind):
        def one(g):
            take_halo(n, g, now[0])
            advance(n + 1, g, now, nxt, *coef[n % 3], kind)

        loop(one)

    sweep(0, even, odd, "first")
    sweep(1, odd, even, "")
    sweep(2, even, odd, "")

    def restrict(g):
        take_halo(3, g, xb)
        apply(g, odd, even, *coef[0], "leftover")
        left = split(jnp.concatenate([ra[g, b] for b in range(rb)], axis=1))
        res = fold(lax.dot_general(left, own_hot[...], NT, preferred_element_type=F32))
        cres[g] = res
        start = cinv[pl.ds(0, 1), :] * res * coef[0][1]
        cout[g] = start
        send_coarse(0, g, start)

    loop(restrict)

    def coarse_sweep(m):
        def one(g):
            arrived(coarse_copy, m, g)
            old = csend[m, g]
            left = jnp.concatenate(
                [split(old)] + [split(crecv[m, g, d]) for d in range(4)], axis=1)
            right = jnp.concatenate([cweight[k] for k in range(5)], axis=1)
            full = fold(lax.dot_general(left, right, NT, preferred_element_type=F32))
            res = cres[g] - (full[:, :bs] + full[:, bs:])
            cres[g] = res
            alpha, beta = coef[m + 1]
            step = alpha * old + beta * (cinv[pl.ds(0, 1), :] * res)
            cout[g] = cout[g] + step
            send_coarse(m + 1, g, step)

        loop(one)

    coarse_sweep(0)
    coarse_sweep(1)
    cor_copy = pltpu.make_async_copy(cout, cor_hbm, out_sem.at[groups])
    cor_copy.start()

    def prolong_own(g):
        left = split(cout[g])
        for b in range(rb):
            part = lax.dot_general(
                left, own_hot[:, pl.ds(b * bs, bs)], NN, preferred_element_type=F32)
            value = fold(part)
            pa[g, b] = value
            xa[g, b] = split(value)

    loop(prolong_own)

    def prolong(g):
        arrived(coarse_copy, 2, g)
        for d in range(4):
            other = crecv[0, g, d] + crecv[1, g, d] + crecv[2, g, d]
            left = split(other)
            for h in range(hb):
                got = lax.dot_general(
                    left, halo_hot[d, :, pl.ds(h * bs, bs)], NN, preferred_element_type=F32)
                xa[g, rb + d * hb + h] = split(fold(got))

    def coarse_back(g):
        prolong(g)
        advance(4, g, even, odd, *coef[0], "")

    loop(coarse_back)
    sweep(4, odd, even, "")

    for d in range(4):
        @pl.when(has[d])
        def _():
            def drain(g):
                for n in range(6):
                    fine_copy(n, g, d).wait_send()
                for m in range(3):
                    coarse_copy(m, g, d).wait_send()

            loop(drain)
            agg_copy(d).wait_send()
    def out_copy(g):
        at = pl.ds(pl.multiple_of(g * vg, vg), vg)
        return pltpu.make_async_copy(x_ref.at[at], sol_hbm.at[at], out_sem.at[g])

    def finish(g):
        take_halo(5, g, xa)
        apply(g, even, None, *coef[2], "last")
        out_copy(g).start()

    loop(finish)

    loop(lambda g: out_copy(g).wait())
    cor_copy.wait()


def carry(sol_in, cor_in, sol_out, cor_out, sem):
    copies = [
        pltpu.make_async_copy(cor_in, cor_out, sem.at[0]),
        pltpu.make_async_copy(sol_in, sol_out, sem.at[1]),
    ]
    for one in copies:
        one.start()
    for one in copies:
        one.wait()


def local(
    right_side, start_guess, fine_matrix, fine_columns, send_lists, aggregates, coarse_matrix,
    n_span, n_stream,
):
    nv, rows = right_side.shape
    rb, nnz, bs, _ = fine_matrix.shape
    hb = send_lists.shape[1] // 4
    groups = GROUPS
    vg = nv // groups
    any_spec = pl.BlockSpec(memory_space=pl.ANY)
    hbm = functools.partial(pltpu.with_memory_space_constraint, memory_space=pltpu.HBM)
    smem = pl.BlockSpec(memory_space=pltpu.SMEM)
    dma = pltpu.SemaphoreType.DMA
    solution, correction = pl.pallas_call(
        functools.partial(kernel, n_span, n_stream, groups, coefficients()),
        out_shape=(
            jax.ShapeDtypeStruct((nv, rows), F32),
            jax.ShapeDtypeStruct((groups, vg, bs), F32),
        ),
        in_specs=[smem, smem] + [any_spec] * 5,
        out_specs=(any_spec, any_spec),
        scratch_shapes=[
            pltpu.VMEM((groups, rb, vg, bs), F32),
            pltpu.VMEM((groups, rb, vg, bs), F32),
            pltpu.VMEM((groups, rb, vg, bs), F32),
            pltpu.VMEM((groups, rb, vg, bs), F32),
            pltpu.VMEM((nv, rows), F32),
            pltpu.VMEM((nv, rows), F32),
            pltpu.VMEM((rb, nnz, bs, bs), BF16),
            pltpu.VMEM((rb, 1, bs), jnp.int32),
            pltpu.VMEM((1, 5, bs, bs), F32),
            pltpu.VMEM((rb, 1, bs), F32),
            pltpu.VMEM((8, bs), F32),
            pltpu.VMEM((groups, rb + 4 * hb, 2 * vg, bs), BF16),
            pltpu.VMEM((groups, rb + 4 * hb, 2 * vg, bs), BF16),
            pltpu.VMEM((6, groups, 4, hb, vg, bs), F32),
            pltpu.VMEM((6, groups, 4, hb, vg, bs), F32),
            pltpu.VMEM((4, hb, 1, bs), jnp.int32),
            pltpu.VMEM((4, hb, 1, bs), jnp.int32),
            pltpu.VMEM((bs, rows), BF16),
            pltpu.VMEM((4, bs, hb * bs), BF16),
            pltpu.VMEM((5, 2 * bs, bs), BF16),
            pltpu.VMEM((3, groups, vg, bs), F32),
            pltpu.VMEM((3, groups, 4, vg, bs), F32),
            pltpu.VMEM((groups, vg, bs), F32),
            pltpu.VMEM((groups, vg, bs), F32),
            pltpu.VMEM((rb, nnz * bs, bs), BF16),
            dma((5,)),
            dma((groups + 1,)),
            dma((9, groups, 4)),
            dma((9, groups, 4)),
            dma((4,)),
            dma((4,)),
        ],
        compiler_params=pltpu.CompilerParams(
            collective_id=0, has_side_effects=True, vmem_limit_bytes=28 * 1024 * 1024),
        name="cycle",
    )(
        hbm(fine_columns.T), hbm(send_lists), hbm(start_guess), hbm(right_side), hbm(fine_matrix),
        hbm(aggregates.reshape(rb, 1, bs)), hbm(coarse_matrix),
    )
    return pl.pallas_call(
        carry,
        out_shape=(
            jax.ShapeDtypeStruct((nv, rows), F32), jax.ShapeDtypeStruct((nv, bs), F32)),
        in_specs=[any_spec, any_spec],
        out_specs=(any_spec, any_spec),
        scratch_shapes=[dma((2,))],
        compiler_params=pltpu.CompilerParams(vmem_limit_bytes=8 * 1024 * 1024),
        name="carry",
    )(solution, correction.reshape(nv, bs))


def solution(mesh):
    placed = (
        P(None, ("span", "stream")),
        P(None, ("span", "stream")),
        P(("span", "stream"), None, None, None),
        P(("span", "stream"), None),
        P(("span", "stream"), None),
        P(("span", "stream")),
        P(("span", "stream"), None, None, None),
    )
    return jax.shard_map(
        functools.partial(local, n_span=mesh.shape["span"], n_stream=mesh.shape["stream"]),
        mesh=mesh,
        in_specs=placed,
        out_specs=(P(None, ("span", "stream")), P(None, ("span", "stream"))),
        check_vma=False,
    )
```

```python
import functools

import jax
import jax.numpy as jnp
from jax import lax
from jax.experimental import pallas as pl
from jax.experimental.pallas import tpu as pltpu
from jax.sharding import PartitionSpec as P

GROUPS = 2
COLUMN = 8

CENTER = 1.1
RADIUS = 0.9
MESH = pl.DeviceIdType.MESH
F32 = jnp.float32
BF16 = jnp.bfloat16
NT = (((1,), (1,)), ((), ()))
NN = (((1,), (0,)), ((), ()))


def coefficients():
    old = RADIUS / CENTER
    pairs = [(0.0, 1.0 / CENTER)]
    for _ in range(2):
        now = 1.0 / (2.0 * CENTER / RADIUS - old)
        pairs.append((now * old, 2.0 * now / RADIUS))
        old = now
    return pairs


def split(value):
    lead = value.astype(BF16).astype(F32)
    return jnp.concatenate([lead, value - lead], axis=0).astype(BF16)


def fold(value):
    half = value.shape[0] // 2
    return value[:half] + value[half:]


def kernel(
    n_span, n_stream, groups, coef,
    cols, lists, x0_hbm, rhs_hbm, mat_hbm, agg_hbm, cmat_hbm,
    sol, cout,
    pa, pb, ra, rb_, rhs, x_ref, mat, agg, cmat, dinv, cinv, xa, xb, send, recv,
    asend, arecv, own_hot, halo_hot, cweight, csend, crecv, cres,
    mat_t, in_sem, ssem, rsem, asem_s, asem_r,
):
    nv, rows = rhs.shape
    vg = nv // groups
    rb, nnz, bs, _ = mat.shape
    hb = send.shape[3]
    span, stream = lax.axis_index("span"), lax.axis_index("stream")
    has = (span > 0, span < n_span - 1, stream > 0, stream < n_stream - 1)
    near = ((span - 1, stream), (span + 1, stream), (span, stream - 1), (span, stream + 1))
    order = (2, 3, 0, 1)

    loads = [
        pltpu.make_async_copy(x0_hbm, x_ref, in_sem.at[0]),
        pltpu.make_async_copy(agg_hbm, agg, in_sem.at[1]),
        pltpu.make_async_copy(mat_hbm, mat, in_sem.at[2]),
        pltpu.make_async_copy(rhs_hbm, rhs, in_sem.at[3]),
        pltpu.make_async_copy(cmat_hbm, cmat, in_sem.at[4]),
    ]
    for one in loads:
        one.start()

    barrier = pltpu.get_barrier_semaphore()
    for d in range(4):
        @pl.when(has[d])
        def _():
            pl.semaphore_signal(barrier, inc=1, device_id=near[d], device_id_type=MESH)

    for d in range(4):
        @pl.when(jnp.logical_not(has[d]))
        def _():
            recv[:, :, d] = jnp.zeros(recv.shape[:2] + recv.shape[3:], F32)
            crecv[:, :, d] = jnp.zeros(crecv.shape[:2] + crecv.shape[3:], F32)
            arecv[d] = jnp.zeros(arecv.shape[1:], jnp.int32)

    peers = sum(one.astype(jnp.int32) for one in has)
    pl.semaphore_wait(barrier, peers)

    def fine_copy(n, g, d):
        return pltpu.make_async_remote_copy(
            src_ref=send.at[n, g, d], dst_ref=recv.at[n, g, d ^ 1],
            send_sem=ssem.at[n, g, d], recv_sem=rsem.at[n, g, d ^ 1],
            device_id=near[d], device_id_type=MESH)

    def coarse_copy(m, g, d):
        return pltpu.make_async_remote_copy(
            src_ref=csend.at[m, g], dst_ref=crecv.at[m, g, d ^ 1],
            send_sem=ssem.at[6 + m, g, d], recv_sem=rsem.at[6 + m, g, d ^ 1],
            device_id=near[d], device_id_type=MESH)

    def agg_copy(d):
        return pltpu.make_async_remote_copy(
            src_ref=asend.at[d], dst_ref=arecv.at[d ^ 1],
            send_sem=asem_s.at[d], recv_sem=asem_r.at[d ^ 1],
            device_id=near[d], device_id_type=MESH)

    def block_of(g, b):
        return (pl.ds(pl.multiple_of(g * vg, vg), vg), pl.ds(b * bs, bs))

    def send_fine(n, g, p, dirs):
        for d in dirs:
            @pl.when(has[d])
            def _():
                for h in range(hb):
                    send[n, g, d, h] = p[g, lists[0, d * hb + h]]
                fine_copy(n, g, d).start()

    def send_coarse(m, g, value):
        csend[m, g] = value
        for d in order:
            @pl.when(has[d])
            def _():
                coarse_copy(m, g, d).start()

    def arrived(copy_of, first, g):
        for d in order:
            @pl.when(has[d])
            def _():
                copy_of(first, g, d ^ 1).wait_recv()

    def loop(body):
        lax.fori_loop(0, groups, lambda g, _: (body(g), 0)[1], 0)

    loads[0].wait()

    def start(g):
        for b in range(rb):
            pa[g, b] = x_ref[block_of(g, b)]
        send_fine(0, g, pa, order)

    loop(start)
    loads[1].wait()
    for d in range(4):
        for h in range(hb):
            asend[d, h] = agg[lists[0, d * hb + h]]
    for d in range(4):
        @pl.when(has[d])
        def _():
            agg_copy(d).start()

    def split_start(g):
        for b in range(rb):
            xa[g, b] = split(x_ref[block_of(g, b)])

    loop(split_start)
    row_id = lax.broadcasted_iota(jnp.int32, (bs, bs), 0)
    lane_id = lax.broadcasted_iota(jnp.int32, (bs, bs), 1)
    eye = row_id == lane_id
    for b in range(rb):
        own_hot[:, pl.ds(b * bs, bs)] = (
            jnp.broadcast_to(agg[b], (bs, bs)) == row_id).astype(F32).astype(BF16)
    loads[2].wait()
    for b in range(rb):
        diag = jnp.sum(jnp.where(eye, mat[b, 0].astype(F32), 0.0), axis=0, keepdims=True)
        dinv[b] = 1.0 / diag
        for k in range(nnz):
            mat_t[b, pl.ds(k * bs, bs), :] = mat[b, k].T
    loads[4].wait()
    cinv[...] = jnp.broadcast_to(
        1.0 / jnp.sum(jnp.where(eye, cmat[0, 0], 0.0), axis=0, keepdims=True), cinv.shape)
    for k in range(5):
        cweight[k] = split(cmat[0, k])
    for d in range(4):
        @pl.when(has[d])
        def _():
            agg_copy(d ^ 1).wait_recv()
        for h in range(hb):
            halo_hot[d, :, pl.ds(h * bs, bs)] = (
                jnp.broadcast_to(arecv[d, h], (bs, bs)) == row_id
            ).astype(F32).astype(BF16)
    loads[3].wait()

    def block_rhs(g):
        for b in range(rb):
            ra[g, b] = rhs[block_of(g, b)]

    loop(block_rhs)

    def take_halo(n, g, x):
        arrived(fine_copy, n, g)
        for d in range(4):
            for h in range(hb):
                x[g, rb + d * hb + h] = split(recv[n, g, d, h])

    def product(g, b, x):
        left = jnp.concatenate([x[g, b]] + [x[g, cols[k, b]] for k in range(1, nnz)], axis=1)
        return fold(lax.dot_general(left, mat_t[b], NN, preferred_element_type=F32))

    def update(g, b, res, p, alpha, beta):
        step = beta * (dinv[b] * res)
        return alpha * p[g, b] + step if alpha else step

    def ahead(n, g, x, p, r, alpha, beta):
        for h in range(hb):
            b = lists[0, far * hb + h]
            send[n, g, far, h] = update(g, b, r[g, b] - product(g, b, x), p, alpha, beta)
        pltpu.make_async_remote_copy(
            src_ref=send.at[n, g, far], dst_ref=recv.at[n, g, 5 - far],
            send_sem=ssem.at[n, g, far], recv_sem=rsem.at[n, g, 5 - far],
            device_id=(span, stream + 2 * far - 5), device_id_type=MESH).start()

    def apply(g, now, nxt, alpha, beta, kind):
        x, p, r = now
        for b in range(rb):
            res = r[g, b] - product(g, b, x)
            at = block_of(g, b)
            if kind == "last":
                sol[at] = x_ref[at] + p[g, b] + update(g, b, res, p, alpha, beta)
                continue
            if kind != "first":
                x_ref[at] = x_ref[at] + p[g, b]
            nxt[2][g, b] = res
            if kind != "leftover":
                step = update(g, b, res, p, alpha, beta)
                nxt[1][g, b] = step
                nxt[0][g, b] = split(step)

    def advance(n, g, now, nxt, alpha, beta, kind):
        @pl.when(edge)
        def _():
            ahead(n, g, *now, alpha, beta)

        apply(g, now, nxt, alpha, beta, kind)
        for d in order:
            @pl.when(jnp.logical_and(has[d], jnp.logical_not(jnp.logical_and(edge, far == d))))
            def _():
                for h in range(hb):
                    send[n, g, d, h] = nxt[1][g, lists[0, d * hb + h]]
                fine_copy(n, g, d).start()

    even, odd = (xa, pa, ra), (xb, pb, rb_)
    low = stream % COLUMN == 0
    far = jnp.where(low, 2, 3)
    edge = jnp.logical_or(
        jnp.logical_and(low, has[2]), jnp.logical_and(stream % COLUMN == COLUMN - 1, has[3]))

    def sweep(n, now, nxt, kind):
        def one(g):
            take_halo(n, g, now[0])
            advance(n + 1, g, now, nxt, *coef[n % 3], kind)

        loop(one)

    sweep(0, even, odd, "first")
    sweep(1, odd, even, "")
    sweep(2, even, odd, "")

    def restrict(g):
        take_halo(3, g, xb)
        apply(g, odd, even, *coef[0], "leftover")
        left = split(jnp.concatenate([ra[g, b] for b in range(rb)], axis=1))
        res = fold(lax.dot_general(left, own_hot[...], NT, preferred_element_type=F32))
        cres[g] = res
        start = cinv[pl.ds(0, 1), :] * res * coef[0][1]
        cout[g] = start
        send_coarse(0, g, start)

    loop(restrict)

    def coarse_sweep(m):
        def one(g):
            arrived(coarse_copy, m, g)
            old = csend[m, g]
            left = jnp.concatenate(
                [split(old)] + [split(crecv[m, g, d]) for d in range(4)], axis=1)
            right = jnp.concatenate([cweight[k] for k in range(5)], axis=1)
            full = fold(lax.dot_general(left, right, NT, preferred_element_type=F32))
            res = cres[g] - (full[:, :bs] + full[:, bs:])
            cres[g] = res
            alpha, beta = coef[m + 1]
            step = alpha * old + beta * (cinv[pl.ds(0, 1), :] * res)
            cout[g] = cout[g] + step
            send_coarse(m + 1, g, step)

        loop(one)

    coarse_sweep(0)
    coarse_sweep(1)
    def prolong_own(g):
        left = split(cout[g])
        for b in range(rb):
            part = lax.dot_general(
                left, own_hot[:, pl.ds(b * bs, bs)], NN, preferred_element_type=F32)
            value = fold(part)
            pa[g, b] = value
            xa[g, b] = split(value)

    loop(prolong_own)

    def prolong(g):
        arrived(coarse_copy, 2, g)
        for d in range(4):
            other = crecv[0, g, d] + crecv[1, g, d] + crecv[2, g, d]
            left = split(other)
            for h in range(hb):
                got = lax.dot_general(
                    left, halo_hot[d, :, pl.ds(h * bs, bs)], NN, preferred_element_type=F32)
                xa[g, rb + d * hb + h] = split(fold(got))

    def coarse_back(g):
        prolong(g)
        advance(4, g, even, odd, *coef[0], "")

    loop(coarse_back)
    sweep(4, odd, even, "")

    for d in range(4):
        @pl.when(has[d])
        def _():
            def drain(g):
                for n in range(6):
                    fine_copy(n, g, d).wait_send()
                for m in range(3):
                    coarse_copy(m, g, d).wait_send()

            loop(drain)
            agg_copy(d).wait_send()
    def finish(g):
        take_halo(5, g, xa)
        apply(g, even, None, *coef[2], "last")

    loop(finish)


def carry(sol_in, cor_in, sol_out, cor_out, sem):
    copies = [
        pltpu.make_async_copy(cor_in, cor_out, sem.at[0]),
        pltpu.make_async_copy(sol_in, sol_out, sem.at[1]),
    ]
    for one in copies:
        one.start()
    for one in copies:
        one.wait()


def local(
    right_side, start_guess, fine_matrix, fine_columns, send_lists, aggregates, coarse_matrix,
    n_span, n_stream,
):
    nv, rows = right_side.shape
    rb, nnz, bs, _ = fine_matrix.shape
    hb = send_lists.shape[1] // 4
    groups = GROUPS
    vg = nv // groups
    any_spec = pl.BlockSpec(memory_space=pl.ANY)
    hbm = functools.partial(pltpu.with_memory_space_constraint, memory_space=pltpu.HBM)
    smem = pl.BlockSpec(memory_space=pltpu.SMEM)
    dma = pltpu.SemaphoreType.DMA
    solution, correction = pl.pallas_call(
        functools.partial(kernel, n_span, n_stream, groups, coefficients()),
        out_shape=(
            jax.ShapeDtypeStruct((nv, rows), F32),
            jax.ShapeDtypeStruct((groups, vg, bs), F32),
        ),
        in_specs=[smem, smem] + [any_spec] * 5,
        out_specs=(pl.BlockSpec(memory_space=pltpu.VMEM),) * 2,
        scratch_shapes=[
            pltpu.VMEM((groups, rb, vg, bs), F32),
            pltpu.VMEM((groups, rb, vg, bs), F32),
            pltpu.VMEM((groups, rb, vg, bs), F32),
            pltpu.VMEM((groups, rb, vg, bs), F32),
            pltpu.VMEM((nv, rows), F32),
            pltpu.VMEM((nv, rows), F32),
            pltpu.VMEM((rb, nnz, bs, bs), BF16),
            pltpu.VMEM((rb, 1, bs), jnp.int32),
            pltpu.VMEM((1, 5, bs, bs), F32),
            pltpu.VMEM((rb, 1, bs), F32),
            pltpu.VMEM((8, bs), F32),
            pltpu.VMEM((groups, rb + 4 * hb, 2 * vg, bs), BF16),
            pltpu.VMEM((groups, rb + 4 * hb, 2 * vg, bs), BF16),
            pltpu.VMEM((6, groups, 4, hb, vg, bs), F32),
            pltpu.VMEM((6, groups, 4, hb, vg, bs), F32),
            pltpu.VMEM((4, hb, 1, bs), jnp.int32),
            pltpu.VMEM((4, hb, 1, bs), jnp.int32),
            pltpu.VMEM((bs, rows), BF16),
            pltpu.VMEM((4, bs, hb * bs), BF16),
            pltpu.VMEM((5, 2 * bs, bs), BF16),
            pltpu.VMEM((3, groups, vg, bs), F32),
            pltpu.VMEM((3, groups, 4, vg, bs), F32),
            pltpu.VMEM((groups, vg, bs), F32),
            pltpu.VMEM((rb, nnz * bs, bs), BF16),
            dma((5,)),
            dma((9, groups, 4)),
            dma((9, groups, 4)),
            dma((4,)),
            dma((4,)),
        ],
        compiler_params=pltpu.CompilerParams(
            collective_id=0, has_side_effects=True, vmem_limit_bytes=28 * 1024 * 1024),
        name="cycle",
    )(
        hbm(fine_columns.T), hbm(send_lists), hbm(start_guess), hbm(right_side), hbm(fine_matrix),
        hbm(aggregates.reshape(rb, 1, bs)), hbm(coarse_matrix),
    )
    return pl.pallas_call(
        carry,
        out_shape=(
            jax.ShapeDtypeStruct((nv, rows), F32), jax.ShapeDtypeStruct((nv, bs), F32)),
        in_specs=[any_spec, any_spec],
        out_specs=(any_spec, any_spec),
        scratch_shapes=[dma((2,))],
        compiler_params=pltpu.CompilerParams(vmem_limit_bytes=8 * 1024 * 1024),
        name="carry",
    )(solution, correction.reshape(nv, bs))


def solution(mesh):
    placed = (
        P(None, ("span", "stream")),
        P(None, ("span", "stream")),
        P(("span", "stream"), None, None, None),
        P(("span", "stream"), None),
        P(("span", "stream"), None),
        P(("span", "stream")),
        P(("span", "stream"), None, None, None),
    )
    return jax.shard_map(
        functools.partial(local, n_span=mesh.shape["span"], n_stream=mesh.shape["stream"]),
        mesh=mesh,
        in_specs=placed,
        out_specs=(P(None, ("span", "stream")), P(None, ("span", "stream"))),
        check_vma=False,
    )
```
